32 devices in a mesh: groups: 2 (over y), wide: 8 (over z, x), mp: 2 (over core).
Axes of the slice: x: 2, y: 2, z: 4, core: 2. Of those that a mesh axis runs over, the one named last changes fastest.
Arguments:
- queries: bfloat16 [2048, 5120], P(('groups', 'wide'), 'mp'), parts along dimension 0, may hold values from -40 to 40
- keys: bfloat16 [2048, 1024], P(('groups', 'wide'), 'mp'), parts along dimension 0, may hold values from -6 to 6
- values: bfloat16 [2048, 1024], P(('groups', 'wide'), 'mp'), parts along dimension 0, may hold values from -6 to 6
- prefix_keys: bfloat16 [2048, 1024], P(('groups', 'wide'), 'mp'), parts along dimension 0, may hold values from -6 to 6
- prefix_values: bfloat16 [2048, 1024], P(('groups', 'wide'), 'mp'), parts along dimension 0, may hold values from -6 to 6
- out_grad: bfloat16 [2048, 5120], P(('groups', 'wide'), 'mp'), parts along dimension 0, may hold values from -96 to 96
- row_prompt: int32 [2048, 1], P(('groups', 'wide')), parts along dimension 0, may hold values from 0 to 7; in each aligned block of 128 rows (0 to 127, 128 to 255, ...) at most 32 rows name the same one
Outputs:
- attn_out: bfloat16 [2048, 5120], P(('groups', 'wide'), 'mp'), parts along dimension 0
- query_grad: bfloat16 [2048, 5120], P(('groups', 'wide'), 'mp'), parts along dimension 0
- key_grad: bfloat16 [2048, 1024], P(('groups', 'wide'), 'mp'), parts along dimension 0
- value_grad: bfloat16 [2048, 1024], P(('groups', 'wide'), 'mp'), parts along dimension 0
- prefix_key_grad: bfloat16 [2048, 1024], P(('groups', 'wide'), 'mp'), parts along dimension 0
- prefix_value_grad: bfloat16 [2048, 1024], P(('groups', 'wide'), 'mp'), parts along dimension 0
The draws below stay inside these ranges and needn't reach their ends.
There are 2 independent parts, one for each index of `groups`. The reference program is written for one: setup_inputs(seed, part) draws one part's arguments, and reference() takes and returns one part's arrays. A program takes and returns all parts, laid end to end along the dimension named above; each array names one. Nothing has to cross between parts.
Inputs may be any that keep to these rules, and one draw needn't show every extreme that they name: `row_prompt`: in every aligned block of 128 rows at most 32 rows name the same prompt, and in some block exactly 32 rows do.
All inputs are finite; a program needn't handle non-finite values.
Results may differ from the reference program's by a relative error of at most 0.024.
Values may be sent and summed in bfloat16 or wider, within the bound.
A program may use at most 128 MiB of HBM per device.

```python
import math
import jax
import jax.numpy as jnp
import numpy as np
from jax import lax

QH = 40
KH = 8
HD = 128
PREFIX = 128
TOK_DEV = 128
GRP = 5
CAP = 32
SLOTS = 256
PROMPTS = 8
ROWS = 1024
N_WIDE = 8


def draw_queries(key, part):
    noise_key = jax.random.fold_in(key, 11)
    return jnp.clip(jax.random.normal(noise_key, (ROWS, QH * HD), jnp.float32), -6.0, 6.0).astype(jnp.bfloat16)


def draw_keys(key, part):
    noise_key = jax.random.fold_in(key, 21)
    return jnp.clip(jax.random.normal(noise_key, (ROWS, KH * HD), jnp.float32), -6.0, 6.0).astype(jnp.bfloat16)


def draw_prefix_keys(key, part):
    noise_key = jax.random.fold_in(key, 31)
    return jnp.clip(jax.random.normal(noise_key, (PROMPTS * PREFIX, KH * HD), jnp.float32), -6.0, 6.0).astype(jnp.bfloat16)


def shard_levels(key, extent, split, least, largest):
    def one(dim, blocks):
        draws = jax.random.uniform(jax.random.fold_in(jax.random.fold_in(key, 6), dim), (blocks,), jnp.float32, least / len(split), largest / len(split))
        return jnp.repeat(jnp.exp(draws), extent[dim] // blocks).reshape((-1,) + (1,) * (len(extent) - dim - 1))

    loudness = one(*split[0])
    for cut in split[1:]:
        loudness = loudness * one(*cut)
    return loudness


def assign_block(key, own, number, rows, count, top, most, slope):
    sequence = jax.random.permutation(key, count)
    crowded, usual = load_shares(count, rows * top, most, slope, True), load_shares(count, rows * top, most, slope, False)
    places = jnp.arange(count)

    def named(tallies, rotation):
        used = int((tallies > 0).sum())
        fixed = max(1, used // 4)
        moved = fixed + (places - fixed + rotation * (used - fixed)) % max(1, count - fixed)
        return jnp.zeros((count,), jnp.int32).at[sequence[jnp.where(places < fixed, places, moved)]].set(jnp.asarray(tallies, jnp.int32))

    tallies = jnp.where(number % 4 == 0, named(crowded, number // 4), named(usual, number - number // 4 - 1))
    mixed = jax.random.permutation(jax.random.fold_in(own, 3), count)
    source_of, sink = mixed[0:count // 2 * 2:2], mixed[1:count // 2 * 2:2]
    slack = jnp.minimum(tallies[source_of] - 1, most - tallies[sink]) // 2
    slack = jnp.where((source_of == sequence[0]) | (sink == sequence[0]) | (tallies[sink] == 0), 0, jnp.maximum(slack, 0))
    moved = jax.random.randint(jax.random.fold_in(own, 4), (count // 2,), 0, 1 << 20) % (slack + 1)
    tallies = tallies.at[source_of].add(-moved).at[sink].add(moved)
    items = jnp.searchsorted(jnp.cumsum(tallies), jnp.arange(rows * top), side="right").astype(jnp.int32)
    listing = items.reshape(top, rows).T
    listing = listing[jax.random.permutation(jax.random.fold_in(own, 1), rows)]
    rotation = jax.random.randint(jax.random.fold_in(own, 2), (rows, 1), 0, top)
    return jnp.take_along_axis(listing, (jnp.arange(top)[None, :] + rotation) % top, axis=1)


def load_shares(count, total, bound, skew, full):
    loads = [(1 << 20) // math.isqrt(grade ** skew) + 1 for grade in range(1, count + 1)]
    largest = bound if full else min(bound, max(-(-total // count), total * loads[0] // sum(loads)))
    least = 1 if total - largest >= count - 1 else 0
    given, surplus = [largest] + [least] * (count - 1), total - largest - least * (count - 1)
    while surplus > 0:
        movable = [i for i in range(1, count) if given[i] < largest] or [i for i in range(1, count) if given[i] < bound]
        mass, remaining = sum([loads[i] for i in movable]), surplus
        for i in movable:
            extra = min(bound - given[i], max(1, remaining * loads[i] // mass), surplus)
            given[i] = given[i] + extra
            surplus = surplus - extra
    return np.array(given)


def gaussian(key, shape, deviation, bound, split=(), held_as=jnp.bfloat16):
    values = deviation * jax.random.normal(key, shape, jnp.float32)
    if split:
        values = values * shard_levels(key, shape, split, -0.22, 0.18)
    return jnp.clip(values, -bound, bound).astype(held_as)


def setup_inputs(seed: int = 0, part: int = 0) -> dict:
    key_of = jax.random.split(jax.random.key(seed), 8)
    part_splits = jax.random.split(jax.random.fold_in(key_of[7], part), 8)
    queries = draw_queries(jax.random.fold_in(jax.random.fold_in(key_of[7], part), 71), part)
    keys = draw_keys(jax.random.fold_in(jax.random.fold_in(key_of[7], part), 71), part)
    values = gaussian(part_splits[2], (ROWS, KH * HD), 1.0, 6.0, ((0, 8), (1, 2)))
    prefix_keys = draw_prefix_keys(jax.random.fold_in(jax.random.fold_in(key_of[7], part), 71), part)
    prefix_values = gaussian(part_splits[4], (PROMPTS * PREFIX, KH * HD), 1.0, 6.0, ((0, 8), (1, 2)))
    out_grad = gaussian(part_splits[5], (ROWS, QH * HD), 16.0, 96.0, ((0, 8), (1, 2)))
    row_prompt_keys = jax.random.split(jax.random.fold_in(part_splits[6], 1), ROWS // TOK_DEV)
    row_prompt_turns = jax.random.permutation(jax.random.fold_in(part_splits[6], 3), ROWS // TOK_DEV)
    row_prompt = jax.vmap(lambda own, number: assign_block(jax.random.fold_in(part_splits[6], 2), own, number, TOK_DEV, N_WIDE, 1, CAP, 1))(row_prompt_keys, row_prompt_turns).reshape((ROWS, 1))
    return dict(queries=queries, keys=keys, values=values, prefix_keys=prefix_keys, prefix_values=prefix_values, out_grad=out_grad, row_prompt=row_prompt)


highest_precision = lax.Precision.HIGHEST


def part_forward(query_heads, key_rows, value_rows, allowed, score_scale):
    outputs, maxima, totals = [], [], []
    for head_group in range(query_heads.shape[1]):
        query_block = query_heads[:, head_group].astype(jnp.float32)
        key_block = key_rows[:, head_group].astype(jnp.float32)
        value_block = value_rows[:, head_group].astype(jnp.float32)
        scores = jnp.einsum("rhd,kd->hrk", query_block, key_block, precision=highest_precision) * score_scale
        if allowed is not None:
            scores = jnp.where(allowed[None], scores, -jnp.inf)
        row_max = jnp.max(scores, axis=2)
        weights = jnp.exp(scores - row_max[:, :, None])
        totals.append(jnp.sum(weights, axis=2))
        maxima.append(row_max)
        rounded = lax.optimization_barrier(weights.astype(jnp.bfloat16)).astype(jnp.float32)
        outputs.append(jnp.einsum("hrk,kd->rhd", rounded, value_block, precision=highest_precision))
    row_count = query_heads.shape[0]
    partial_value = jnp.stack(outputs, axis=1).reshape(row_count, -1)
    return partial_value, jnp.concatenate(maxima, axis=0).T, jnp.concatenate(totals, axis=0).T


def part_backward(query_heads, key_rows, value_rows, allowed, score_scale, grad_heads, log_total, row_delta):
    group_size = query_heads.shape[2]
    query_parts, key_parts, value_parts = [], [], []
    for head_group in range(query_heads.shape[1]):
        first = head_group * group_size
        query_block = query_heads[:, head_group].astype(jnp.float32)
        key_block = key_rows[:, head_group].astype(jnp.float32)
        value_block = value_rows[:, head_group].astype(jnp.float32)
        grad_block = grad_heads[:, head_group].astype(jnp.float32)
        scores = jnp.einsum("rhd,kd->hrk", query_block, key_block, precision=highest_precision) * score_scale
        if allowed is not None:
            scores = jnp.where(allowed[None], scores, -jnp.inf)
        group_total = log_total[:, first:first + group_size].T
        group_delta = row_delta[:, first:first + group_size].T
        probs = jnp.exp(scores - group_total[:, :, None])
        probs_low = lax.optimization_barrier(probs.astype(jnp.bfloat16)).astype(jnp.float32)
        value_parts.append(jnp.einsum("hrk,rhd->kd", probs_low, grad_block, precision=highest_precision))
        dprob = jnp.einsum("rhd,kd->hrk", grad_block, value_block, precision=highest_precision)
        dscore = probs * (dprob - group_delta[:, :, None])
        dscore = lax.optimization_barrier(dscore.astype(jnp.bfloat16)).astype(jnp.float32)
        query_parts.append(jnp.einsum("hrk,kd->rhd", dscore, key_block, precision=highest_precision) * score_scale)
        key_parts.append(jnp.einsum("hrk,rhd->kd", dscore, query_block, precision=highest_precision) * score_scale)
    row_count = query_heads.shape[0]
    key_count = key_rows.shape[0]
    return (jnp.stack(query_parts, axis=1).reshape(row_count, -1),
            jnp.stack(key_parts, axis=1).reshape(key_count, -1),
            jnp.stack(value_parts, axis=1).reshape(key_count, -1))


def merge_parts(first_out, first_max, first_total, second_out, second_max, second_total, head_size):
    joint_max = jnp.maximum(first_max, second_max)
    first_factor = jnp.exp(first_max - joint_max)
    second_factor = jnp.exp(second_max - joint_max)
    joint_total = first_factor * first_total + second_factor * second_total
    row_count, head_count = first_max.shape
    combined = (first_out.reshape(row_count, head_count, head_size) * first_factor[:, :, None]
                + second_out.reshape(row_count, head_count, head_size) * second_factor[:, :, None]) / joint_total[:, :, None]
    return combined.reshape(row_count, head_count * head_size).astype(jnp.bfloat16), joint_max + jnp.log(joint_total)


def out_delta(grad_rows, out_rows, head_size):
    row_count = grad_rows.shape[0]
    product = grad_rows.astype(jnp.float32) * out_rows.astype(jnp.float32)
    return jnp.sum(product.reshape(row_count, -1, head_size), axis=2)


def reference(queries, keys, values, prefix_keys, prefix_values, out_grad, row_prompt):
    score_scale = HD ** -0.5
    prompt = row_prompt[:, 0]
    positions = jnp.arange(TOK_DEV, dtype=jnp.int32)
    causal = positions[None, :] <= positions[:, None]

    def own_allowed(prompt_block):
        return (prompt_block[:, None] == prompt_block[None, :]) & causal

    def own_forward(block):
        query_block, key_block, value_block, prompt_block = block
        return part_forward(query_block.reshape(TOK_DEV, KH, GRP, HD), key_block.reshape(TOK_DEV, KH, HD),
                            value_block.reshape(TOK_DEV, KH, HD), own_allowed(prompt_block), score_scale)

    device_queries = queries.reshape(N_WIDE, TOK_DEV, QH * HD)
    device_keys = keys.reshape(N_WIDE, TOK_DEV, KH * HD)
    device_values = values.reshape(N_WIDE, TOK_DEV, KH * HD)
    device_prompt = prompt.reshape(N_WIDE, TOK_DEV)
    own_out, own_max, own_total = lax.map(own_forward, (device_queries, device_keys, device_values, device_prompt))
    own_out = own_out.reshape(ROWS, QH * HD)
    own_max = own_max.reshape(ROWS, QH)
    own_total = own_total.reshape(ROWS, QH)

    sorted_rows = jnp.argsort(prompt, stable=True).astype(jnp.int32)
    owner_ids = jnp.arange(PROMPTS, dtype=jnp.int32)
    counts = jnp.sum((prompt[:, None] == owner_ids[None, :]).astype(jnp.int32), axis=0)
    starts = (jnp.cumsum(counts) - counts).astype(jnp.int32)
    padded_rows = jnp.concatenate([sorted_rows, jnp.zeros((SLOTS,), jnp.int32)])
    slot_range = jnp.arange(SLOTS, dtype=jnp.int32)

    def owner_rows(owner_id):
        picked = lax.dynamic_slice(padded_rows, (starts[owner_id],), (SLOTS,))
        filled = slot_range < counts[owner_id]
        return picked, filled[:, None]

    def owner_prefix(owner_id):
        key_block = lax.dynamic_slice_in_dim(prefix_keys, owner_id * PREFIX, PREFIX, 0).reshape(PREFIX, KH, HD)
        value_block = lax.dynamic_slice_in_dim(prefix_values, owner_id * PREFIX, PREFIX, 0).reshape(PREFIX, KH, HD)
        return key_block, value_block

    def prefix_forward(carry, owner_id):
        out_acc, max_acc, total_acc = carry
        picked, filled = owner_rows(owner_id)
        query_block = jnp.where(filled, queries[picked], jnp.zeros((), queries.dtype))
        key_block, value_block = owner_prefix(owner_id)
        partial_value, row_max, row_total = part_forward(query_block.reshape(SLOTS, KH, GRP, HD), key_block, value_block,
                                                   None, score_scale)
        return (out_acc.at[picked].add(jnp.where(filled, partial_value, 0.0)),
                max_acc.at[picked].add(jnp.where(filled, row_max, 0.0)),
                total_acc.at[picked].add(jnp.where(filled, row_total, 0.0))), None

    start_carry = (jnp.zeros((ROWS, QH * HD), jnp.float32), jnp.zeros((ROWS, QH), jnp.float32),
                   jnp.zeros((ROWS, QH), jnp.float32))
    (prefix_out, prefix_max, prefix_total), _ = lax.scan(prefix_forward, start_carry, owner_ids)

    attn_out, log_total = merge_parts(prefix_out, prefix_max, prefix_total, own_out, own_max, own_total, HD)
    row_delta = out_delta(out_grad, attn_out, HD)

    def prefix_backward(carry, owner_id):
        picked, filled = owner_rows(owner_id)
        query_block = jnp.where(filled, queries[picked], jnp.zeros((), queries.dtype))
        grad_block = jnp.where(filled, out_grad[picked], jnp.zeros((), out_grad.dtype))
        total_block = jnp.where(filled, log_total[picked], 0.0)
        delta_block = jnp.where(filled, row_delta[picked], 0.0)
        key_block, value_block = owner_prefix(owner_id)
        query_part, key_part, value_part = part_backward(
            query_block.reshape(SLOTS, KH, GRP, HD), key_block, value_block, None, score_scale,
            grad_block.reshape(SLOTS, KH, GRP, HD), total_block, delta_block)
        return carry.at[picked].add(jnp.where(filled, query_part, 0.0)), (key_part, value_part)

    prefix_query, (prefix_key, prefix_value) = lax.scan(prefix_backward, jnp.zeros((ROWS, QH * HD), jnp.float32),
                                                         owner_ids)

    def own_backward(block):
        query_block, key_block, value_block, prompt_block, grad_block, total_block, delta_block = block
        return part_backward(query_block.reshape(TOK_DEV, KH, GRP, HD), key_block.reshape(TOK_DEV, KH, HD),
                             value_block.reshape(TOK_DEV, KH, HD), own_allowed(prompt_block), score_scale,
                             grad_block.reshape(TOK_DEV, KH, GRP, HD), total_block, delta_block)

    own_query, own_key, own_value = lax.map(own_backward, (
        device_queries, device_keys, device_values, device_prompt, out_grad.reshape(N_WIDE, TOK_DEV, QH * HD),
        log_total.reshape(N_WIDE, TOK_DEV, QH), row_delta.reshape(N_WIDE, TOK_DEV, QH)))
    rounded_prefix = lax.optimization_barrier(prefix_query.astype(jnp.bfloat16)).astype(jnp.float32)
    query_grad = (rounded_prefix + own_query.reshape(ROWS, QH * HD)).astype(jnp.bfloat16)
    return (attn_out, query_grad,
            own_key.reshape(ROWS, KH * HD).astype(jnp.bfloat16),
            own_value.reshape(ROWS, KH * HD).astype(jnp.bfloat16),
            prefix_key.reshape(PROMPTS * PREFIX, KH * HD).astype(jnp.bfloat16),
            prefix_value.reshape(PROMPTS * PREFIX, KH * HD).astype(jnp.bfloat16))
```

```python
import functools

import jax
import jax.numpy as jnp
from jax import lax
from jax.experimental import pallas as pl
from jax.experimental.pallas import tpu as pltpu
from jax.sharding import PartitionSpec as P

QH = 40
KH = 8
HD = 128
GRP = QH // KH
MASKED = -1e30


def nt(a, b):
    return lax.dot_general(a, b, (((1,), (1,)), ((), ())), preferred_element_type=jnp.float32)


def nn(a, b):
    return lax.dot_general(a, b, (((1,), (0,)), ((), ())), preferred_element_type=jnp.float32)


def tn(a, b):
    return lax.dot_general(a, b, (((0,), (0,)), ((), ())), preferred_element_type=jnp.float32)


def row_slots(prompt, n_wide, capacity):
    rows = prompt.shape[0]
    lanes = max(128, n_wide)
    hits = prompt == lax.broadcasted_iota(jnp.int32, (rows, lanes), 1)
    earlier = lax.broadcasted_iota(jnp.int32, (rows, rows), 1) < lax.broadcasted_iota(
        jnp.int32, (rows, rows), 0
    )
    seen = nn(
        jnp.where(earlier, 1.0, 0.0).astype(jnp.bfloat16),
        jnp.where(hits, 1.0, 0.0).astype(jnp.bfloat16),
    )
    rank = jnp.sum(jnp.where(hits, seen, 0.0), axis=1, keepdims=True)
    slot = prompt.astype(jnp.float32) * capacity + rank
    places = lax.broadcasted_iota(jnp.int32, (rows, n_wide * capacity), 1).astype(jnp.float32)
    return jnp.where(slot == places, 1.0, 0.0).astype(jnp.bfloat16)


def key_mask(keys, slots, capacity, prefix_rows, bunch):
    shape = (keys, GRP * slots)
    key = lax.broadcasted_iota(jnp.int32, shape, 0)
    row = lax.broadcasted_iota(jnp.int32, shape, 1) % slots
    own = key - bunch * prefix_rows
    same = jnp.where(own >= 0, own // capacity, key // prefix_rows) == row // capacity
    return same & (own <= row)


def attend(q, g, k, v, mask, masked_rows, scale):
    keys = k.shape[0]
    scores = nt(k, q) * scale
    if masked_rows == keys:
        scores = jnp.where(mask, scores, MASKED)
    else:
        scores = jnp.concatenate(
            [
                scores[: keys - masked_rows],
                jnp.where(mask[keys - masked_rows :], scores[keys - masked_rows :], MASKED),
            ],
            axis=0,
        )
    weights = jnp.exp(scores - jnp.max(scores, axis=0, keepdims=True))
    probs = weights * (1.0 / jnp.sum(weights, axis=0, keepdims=True))
    low = probs.astype(jnp.bfloat16)
    dprob = nt(v, g)
    weighted = probs * dprob
    delta = jnp.sum(weighted, axis=0, keepdims=True)
    dscore = (weighted - probs * delta).astype(jnp.bfloat16)
    return tn(low, v), tn(dscore, k) * scale, nn(dscore, q) * scale, nn(low, g)


def group_step(n_wide, capacity, slots, select, q, g, k, v, prefix_of, o_ref, dq_ref, dk_ref, dv_ref, put_prefix):
    scale = HD ** (-0.5)
    bunch = slots // capacity
    tiles = n_wide * capacity // slots
    bf = jnp.bfloat16
    qs, gs, ks, vs = (tn(select, x).astype(bf) for x in (q, g, k, v))
    outs, dqs, dks, dvs = [], [], [], []
    for t in range(tiles):
        span = slice(t * slots, (t + 1) * slots)
        pk, pv = prefix_of(t * bunch, bunch)
        prefix_rows = pk.shape[0] // bunch
        stack = lambda x: jnp.concatenate(
            [x[span, h * HD : (h + 1) * HD] for h in range(GRP)], axis=0
        )
        key_block = jnp.concatenate([pk, ks[span]], axis=0)
        value_block = jnp.concatenate([pv, vs[span]], axis=0)
        keys = key_block.shape[0]
        mask = key_mask(keys, slots, capacity, prefix_rows, bunch)
        out, dq, dk, dv = attend(
            stack(qs), stack(gs), key_block, value_block, mask, slots if bunch == 1 else keys, scale
        )
        unstack = lambda x: jnp.concatenate(
            [x[h * slots : (h + 1) * slots] for h in range(GRP)], axis=1
        ).astype(bf)
        outs.append(unstack(out))
        dqs.append(unstack(dq))
        split = bunch * prefix_rows
        put_prefix(t * bunch, bunch, dk[:split].astype(bf), dv[:split].astype(bf))
        dks.append(dk[split:].astype(bf))
        dvs.append(dv[split:].astype(bf))
    for ref, parts in ((o_ref, outs), (dq_ref, dqs), (dk_ref, dks), (dv_ref, dvs)):
        ref[...] = nn(select, jnp.concatenate(parts, axis=0)).astype(bf)


def kernel(n_wide, capacity, slots, prompt, q, g, k, v, pk, pv, o, dq, dk, dv, pdk, pdv, select):
    @pl.when(pl.program_id(0) == 0)
    def _():
        select[...] = row_slots(prompt[...], n_wide, capacity)

    prefix_rows = pk.shape[0] // n_wide

    def prefix_of(first, count):
        span = pl.ds(first * prefix_rows, count * prefix_rows)
        return pk[span, :], pv[span, :]

    def put_prefix(first, count, dkey, dvalue):
        span = pl.ds(first * prefix_rows, count * prefix_rows)
        pdk[span, :] = dkey
        pdv[span, :] = dvalue

    group_step(
        n_wide, capacity, slots, select[...], q[...], g[...], k[...], v[...], prefix_of, o, dq, dk, dv, put_prefix
    )


def per_device(queries, keys, values, prefix_keys, prefix_values, out_grad, row_prompt):
    n_wide = lax.axis_size("wide")
    rows = queries.shape[0]
    capacity = 2 * rows // n_wide
    slots = max(32, capacity)
    groups = keys.shape[1] // HD
    gather = lambda x: lax.all_gather(x, "wide", axis=0, tiled=True)
    pk, pv = gather(prefix_keys), gather(prefix_values)
    wide_rows = pk.shape[0]
    col = lambda r, c: pl.BlockSpec((r, c), lambda i: (0, i))
    shape = lambda x: jax.ShapeDtypeStruct(x.shape, jnp.bfloat16)
    o, dq, dk, dv, pdk, pdv = pl.pallas_call(
        functools.partial(kernel, n_wide, capacity, slots),
        grid=(groups,),
        out_shape=[shape(x) for x in (queries, queries, keys, values, pk, pv)],
        in_specs=[
            pl.BlockSpec((rows, 1), lambda i: (0, 0)),
            col(rows, GRP * HD),
            col(rows, GRP * HD),
            col(rows, HD),
            col(rows, HD),
            col(wide_rows, HD),
            col(wide_rows, HD),
        ],
        out_specs=[
            col(rows, GRP * HD),
            col(rows, GRP * HD),
            col(rows, HD),
            col(rows, HD),
            col(wide_rows, HD),
            col(wide_rows, HD),
        ],
        scratch_shapes=[pltpu.VMEM((rows, n_wide * capacity), jnp.bfloat16)],
    )(row_prompt, queries, out_grad, keys, values, pk, pv)
    scatter = lambda x: lax.psum_scatter(x, "wide", scatter_dimension=0, tiled=True)
    return o, dq, dk, dv, scatter(pdk), scatter(pdv)


def solution(mesh):
    rows = P(("groups", "wide"), "mp")
    return jax.shard_map(
        per_device,
        mesh=mesh,
        in_specs=(rows,) * 6 + (P(("groups", "wide"), None),),
        out_specs=(rows,) * 6,
        check_vma=False,
    )
```

```python
import functools

import jax
import jax.numpy as jnp
from jax import lax
from jax.experimental import pallas as pl
from jax.experimental.pallas import tpu as pltpu
from jax.sharding import PartitionSpec as P

QH = 40
KH = 8
HD = 128
GRP = QH // KH
MASKED = -1e30


def nt(a, b):
    return lax.dot_general(a, b, (((1,), (1,)), ((), ())), preferred_element_type=jnp.float32)


def nn(a, b):
    return lax.dot_general(a, b, (((1,), (0,)), ((), ())), preferred_element_type=jnp.float32)


def tn(a, b):
    return lax.dot_general(a, b, (((0,), (0,)), ((), ())), preferred_element_type=jnp.float32)


def row_slots(prompt, n_wide, capacity):
    rows = prompt.shape[0]
    lanes = max(128, n_wide)
    hits = prompt == lax.broadcasted_iota(jnp.int32, (rows, lanes), 1)
    earlier = lax.broadcasted_iota(jnp.int32, (rows, rows), 1) < lax.broadcasted_iota(
        jnp.int32, (rows, rows), 0
    )
    seen = nn(
        jnp.where(earlier, 1.0, 0.0).astype(jnp.bfloat16),
        jnp.where(hits, 1.0, 0.0).astype(jnp.bfloat16),
    )
    rank = jnp.sum(jnp.where(hits, seen, 0.0), axis=1, keepdims=True)
    slot = prompt.astype(jnp.float32) * capacity + rank
    places = lax.broadcasted_iota(jnp.int32, (rows, n_wide * capacity), 1).astype(jnp.float32)
    return jnp.where(slot == places, 1.0, 0.0).astype(jnp.bfloat16)


def key_mask(keys, slots, capacity, prefix_rows, bunch):
    shape = (keys, GRP * slots)
    key = lax.broadcasted_iota(jnp.int32, shape, 0)
    row = lax.broadcasted_iota(jnp.int32, shape, 1) % slots
    own = key - bunch * prefix_rows
    same = jnp.where(own >= 0, own // capacity, key // prefix_rows) == row // capacity
    return same & (own <= row)


def attend(q, g, k, v, mask, masked_rows, scale):
    keys = k.shape[0]
    scores = nt(k, q) * scale
    if masked_rows == keys:
        scores = jnp.where(mask, scores, MASKED)
    else:
        scores = jnp.concatenate(
            [
                scores[: keys - masked_rows],
                jnp.where(mask[keys - masked_rows :], scores[keys - masked_rows :], MASKED),
            ],
            axis=0,
        )
    weights = jnp.exp(scores - jnp.max(scores, axis=0, keepdims=True))
    probs = weights * (1.0 / jnp.sum(weights, axis=0, keepdims=True))
    low = probs.astype(jnp.bfloat16)
    dprob = nt(v, g)
    weighted = probs * dprob
    delta = jnp.sum(weighted, axis=0, keepdims=True)
    dscore = (weighted - probs * delta).astype(jnp.bfloat16)
    return tn(low, v), tn(dscore, k) * scale, nn(dscore, q) * scale, nn(low, g)


def ring_index(position, count):
    half = count // 2
    position = lax.rem(position + 2 * count, count)
    return jnp.where(position < half, 2 * position, 2 * (count - 1 - position) + 1)


def ring_position(index, count):
    return jnp.where(index % 2 == 0, index // 2, count - 1 - index // 2)


def kernel(
    n, capacity, slots, groups,
    prompt, q, g, k, v, pk, pv, o, dq, dk, dv, pdk, pdv,
    kv, part, landed, qs, gs, ks, vs, os, dqs, dks, dvs,
    own_sem, ag_send, ag_recv, rs_send, rs_recv,
):
    bf = jnp.bfloat16
    scale = HD ** (-0.5)
    half = n // 2
    bunch = slots // capacity
    tiles = n * capacity // slots
    rows = pk.shape[0]
    width = GRP * HD
    me = lax.axis_index("wide")
    here = ring_position(me, n)
    at = lambda offset: ring_index(here + offset, n)
    right, left = at(1), at(-1)
    copies = []

    own = []
    for c in range(groups):
        for part_id, ref in enumerate((pk, pv)):
            copy = pltpu.make_async_copy(
                ref.at[:, pl.ds(c * HD, HD)],
                kv.at[me, c, pl.ds(part_id * rows, rows)],
                own_sem.at[c, part_id],
            )
            copy.start()
            own.append(copy)

    barrier = pltpu.get_barrier_semaphore()
    for other in (left, right):
        pl.semaphore_signal(
            barrier, inc=1, device_id={"wide": other}, device_id_type=pl.DeviceIdType.MESH
        )
    pl.semaphore_wait(barrier, 2)

    def send(src, dst, send_sem, recv_sem, device):
        return pltpu.make_async_remote_copy(
            src_ref=src,
            dst_ref=dst,
            send_sem=send_sem,
            recv_sem=recv_sem,
            device_id={"wide": device},
            device_id_type=pl.DeviceIdType.MESH,
        )

    def span(way, short):
        return pl.ds(way * rows, rows) if short else pl.ds(0, 2 * rows)

    def gather_copy(way, c, s):
        sign = 1 - 2 * way
        block = kv.at[at(-sign * (s - 1)), c, span(way, s == half)]
        return send(
            block, block, ag_send.at[way, c, s - 1], ag_recv.at[way, c, s - 1], (right, left)[way]
        )

    def gather(c, s):
        if s == 0:
            own[2 * c].wait()
            own[2 * c + 1].wait()
        for way in range(2):
            if s > 0:
                gather_copy(way, c, s).wait_recv()
            if s < half:
                copy = gather_copy(way, c, s + 1)
                copy.start()
                copies.append(copy)

    def reduce_copy(way, c, s):
        sign = 1 - 2 * way
        part_of = span(way, s == 1)
        return send(
            part.at[at(sign * (half + 1 - s)), c, part_of],
            landed.at[way, c, s - 1, part_of],
            rs_send.at[way, c, s - 1],
            rs_recv.at[way, c, s - 1],
            (right, left)[way],
        )

    def reduce(c, s):
        for way in range(2):
            sign = 1 - 2 * way
            if s > 1:
                reduce_copy(way, c, s - 1).wait_recv()
            if s <= half:
                if s > 1:
                    part_of = span(way, s == 2)
                    target = at(sign * (half + 1 - s))
                    part[target, c, part_of] = (
                        part[target, c, part_of].astype(jnp.float32)
                        + landed[way, c, s - 2, part_of].astype(jnp.float32)
                    ).astype(bf)
                copy = reduce_copy(way, c, s)
                copy.start()
                copies.append(copy)
        if s > half:
            for part_id, ref in enumerate((pdk, pdv)):
                part_of = pl.ds(part_id * rows, rows)
                total = part[me, c, part_of].astype(jnp.float32)
                for way in range(2):
                    if half > 1 or way == part_id:
                        total += landed[way, c, half - 1, part_of].astype(jnp.float32)
                ref[:, pl.ds(c * HD, HD)] = total.astype(bf)

    waits = sorted((c + s, c, s) for c in range(groups) for s in range(half + 1))
    for tick, c, s in [w for w in waits if w[0] < 2]:
        gather(c, s)
    waits = [w for w in waits if w[0] >= 2]

    select = row_slots(prompt[...], n, capacity)
    for src, dst in ((k, ks), (v, vs)):
        dst[...] = tn(select, src[...]).astype(bf)

    def to_slots(c):
        for src, dst in ((q, qs), (g, gs)):
            dst[:, c * width : (c + 1) * width] = tn(select, src[:, c * width : (c + 1) * width]).astype(bf)

    to_slots(0)
    ready = 1

    def from_slots(c):
        for slot_ref, ref, cols in ((os, o, width), (dqs, dq, width), (dks, dk, HD), (dvs, dv, HD)):
            ref[:, c * cols : (c + 1) * cols] = nn(select, slot_ref[...]).astype(bf)

    keys = bunch * rows + slots
    mask = key_mask(keys, slots, capacity, rows, bunch)
    ahead = [half]
    for step in range(half - 1, 0, -1):
        ahead += [step, -step]
    ahead += [0]

    def tile(c, t):
        first = at(ahead[t]) if bunch == 1 else t * bunch
        place = pl.ds(pl.multiple_of(first * capacity, slots), slots)
        stack = lambda ref: jnp.concatenate(
            [ref[place, c * width + h * HD : c * width + (h + 1) * HD] for h in range(GRP)], axis=0
        )
        cols = slice(c * HD, (c + 1) * HD)
        key_block = jnp.concatenate(
            [kv[first + i, c, :rows] for i in range(bunch)] + [ks[place, cols]], axis=0
        )
        value_block = jnp.concatenate(
            [kv[first + i, c, rows:] for i in range(bunch)] + [vs[place, cols]], axis=0
        )
        out, dquery, dkey, dvalue = attend(
            stack(qs), stack(gs), key_block, value_block, mask, slots if bunch == 1 else keys, scale
        )
        for ref, value in ((os, out), (dqs, dquery)):
            for h in range(GRP):
                ref[place, h * HD : (h + 1) * HD] = value[h * slots : (h + 1) * slots].astype(bf)
        for i in range(bunch):
            piece = slice(i * rows, (i + 1) * rows)
            part[first + i, c, :rows] = dkey[piece].astype(bf)
            part[first + i, c, rows:] = dvalue[piece].astype(bf)
        dks[place, :] = dkey[bunch * rows :].astype(bf)
        dvs[place, :] = dvalue[bunch * rows :].astype(bf)

    reduces = []
    for c in range(groups):
        reduces.append((c * tiles + (0 if bunch == 1 else tiles - 1), c, 1))
        for s in range(2, half + 2):
            reduces.append((c * tiles + tiles - 1 + 5 * (s - 2), c, s))
    reduces.sort()

    for c in range(groups):
        while waits and waits[0][:2] <= (half + c, c):
            tick, other, s = waits.pop(0)
            gather(other, s)
            if ready < groups:
                to_slots(ready)
                ready += 1
        while ready < min(groups, c + 2):
            to_slots(ready)
            ready += 1
        for t in range(tiles):
            tile(c, t)
            if t % 2 == 0 and waits and waits[0][0] <= half + c:
                tick, other, s = waits.pop(0)
                gather(other, s)
            while reduces and reduces[0][0] <= c * tiles + t:
                _, other, s = reduces.pop(0)
                reduce(other, s)
        from_slots(c)
    for _, other, s in reduces:
        reduce(other, s)
    for copy in copies:
        copy.wait_send()


def per_device(queries, keys, values, prefix_keys, prefix_values, out_grad, row_prompt):
    n = lax.axis_size("wide")
    rows = queries.shape[0]
    prefix_rows = prefix_keys.shape[0]
    capacity = 2 * rows // n
    slots = max(32, capacity)
    places = n * capacity
    groups = keys.shape[1] // HD
    half = n // 2
    bf = jnp.bfloat16
    shape = lambda x: jax.ShapeDtypeStruct(x.shape, bf)
    vmem = pl.BlockSpec(memory_space=pltpu.VMEM)
    anywhere = pl.BlockSpec(memory_space=pl.ANY)
    sems = pltpu.SemaphoreType.DMA
    return pl.pallas_call(
        functools.partial(kernel, n, capacity, slots, groups),
        out_shape=[shape(x) for x in (queries, queries, keys, values, prefix_keys, prefix_values)],
        in_specs=[vmem] * 5 + [anywhere] * 2,
        out_specs=[vmem] * 6,
        scratch_shapes=[
            pltpu.VMEM((n, groups, 2 * prefix_rows, HD), bf),
            pltpu.VMEM((n, groups, 2 * prefix_rows, HD), bf),
            pltpu.VMEM((2, groups, half, 2 * prefix_rows, HD), bf),
            pltpu.VMEM((places, queries.shape[1]), bf),
            pltpu.VMEM((places, queries.shape[1]), bf),
            pltpu.VMEM((places, keys.shape[1]), bf),
            pltpu.VMEM((places, keys.shape[1]), bf),
            pltpu.VMEM((places, GRP * HD), bf),
            pltpu.VMEM((places, GRP * HD), bf),
            pltpu.VMEM((places, HD), bf),
            pltpu.VMEM((places, HD), bf),
            sems((groups, 2)),
            sems((2, groups, half)),
            sems((2, groups, half)),
            sems((2, groups, half)),
            sems((2, groups, half)),
        ],
        compiler_params=pltpu.CompilerParams(collective_id=0, has_side_effects=True),
    )(row_prompt, queries, out_grad, keys, values, prefix_keys, prefix_values)


def solution(mesh):
    rows = P(("groups", "wide"), "mp")
    return jax.shard_map(
        per_device,
        mesh=mesh,
        in_specs=(rows,) * 6 + (P(("groups", "wide"), None),),
        out_specs=(rows,) * 6,
        check_vma=False,
    )
```

```python
import functools

import jax
import jax.numpy as jnp
from jax import lax
from jax.experimental import pallas as pl
from jax.experimental.pallas import tpu as pltpu
from jax.sharding import PartitionSpec as P

QH = 40
KH = 8
HD = 128
GRP = QH // KH
MASKED = -1e30
LEAD = 2
EARLY = 4
GAP = 12


def nt(a, b):
    return lax.dot_general(a, b, (((1,), (1,)), ((), ())), preferred_element_type=jnp.float32)


def nn(a, b):
    return lax.dot_general(a, b, (((1,), (0,)), ((), ())), preferred_element_type=jnp.float32)


def tn(a, b):
    return lax.dot_general(a, b, (((0,), (0,)), ((), ())), preferred_element_type=jnp.float32)


def row_slots(prompt, n_wide, capacity):
    rows = prompt.shape[1]
    lanes = max(128, n_wide)
    prompt = jnp.broadcast_to(prompt.astype(jnp.float32), (128, rows)).T[:, :1].astype(jnp.int32)
    hits = prompt == lax.broadcasted_iota(jnp.int32, (rows, lanes), 1)
    earlier = lax.broadcasted_iota(jnp.int32, (rows, rows), 1) < lax.broadcasted_iota(
        jnp.int32, (rows, rows), 0
    )
    seen = nn(
        jnp.where(earlier, 1.0, 0.0).astype(jnp.bfloat16),
        jnp.where(hits, 1.0, 0.0).astype(jnp.bfloat16),
    )
    rank = jnp.sum(jnp.where(hits, seen, 0.0), axis=1, keepdims=True)
    slot = prompt.astype(jnp.float32) * capacity + rank
    places = lax.broadcasted_iota(jnp.int32, (rows, n_wide * capacity), 1).astype(jnp.float32)
    return jnp.where(slot == places, 1.0, 0.0).astype(jnp.bfloat16)


def key_mask(keys, slots, capacity, prefix_rows, bunch):
    shape = (keys, GRP * slots)
    key = lax.broadcasted_iota(jnp.int32, shape, 0)
    row = lax.broadcasted_iota(jnp.int32, shape, 1) % slots
    own = key - bunch * prefix_rows
    same = jnp.where(own >= 0, own // capacity, key // prefix_rows) == row // capacity
    return same & (own <= row)


def attend(q, g, k, v, mask, masked_rows, scale):
    keys = k.shape[0]
    scores = nt(k, q) * scale
    if masked_rows == keys:
        scores = jnp.where(mask, scores, MASKED)
    else:
        scores = jnp.concatenate(
            [
                scores[: keys - masked_rows],
                jnp.where(mask[keys - masked_rows :], scores[keys - masked_rows :], MASKED),
            ],
            axis=0,
        )
    weights = jnp.exp(scores - jnp.max(scores, axis=0, keepdims=True))
    probs = weights * (1.0 / jnp.sum(weights, axis=0, keepdims=True))
    low = probs.astype(jnp.bfloat16)
    dprob = nt(v, g)
    weighted = probs * dprob
    delta = jnp.sum(weighted, axis=0, keepdims=True)
    dscore = (weighted - probs * delta).astype(jnp.bfloat16)
    return tn(low, v), tn(dscore, k) * scale, nn(dscore, q) * scale, nn(low, g)


def ring_index(position, count):
    half = count // 2
    position = lax.rem(position + 2 * count, count)
    return jnp.where(position < half, 2 * position, 2 * (count - 1 - position) + 1)


def ring_position(index, count):
    return jnp.where(index % 2 == 0, index // 2, count - 1 - index // 2)


def kernel(
    n, capacity, slots, groups,
    prompt, q_far, g_far, k, v, pk, pv, o, dq, dk, dv, pdk, pdv,
    q, g, kv, part, landed, qs, gs, ks, vs, os, dqs, dks, dvs,
    in_sem, own_sem, ag_send, ag_recv, rs_send, rs_recv,
):
    bf = jnp.bfloat16
    scale = HD ** (-0.5)
    half = n // 2
    bunch = slots // capacity
    tiles = n * capacity // slots
    rows = pk.shape[0]
    width = GRP * HD
    me = lax.axis_index("wide")
    here = ring_position(me, n)
    at = lambda offset: ring_index(here + offset, n)
    right, left = at(1), at(-1)
    copies = []

    own = []
    for c in range(groups):
        for part_id, ref in enumerate((pk, pv)):
            copy = pltpu.make_async_copy(
                ref.at[:, pl.ds(c * HD, HD)],
                kv.at[me, c, pl.ds(part_id * rows, rows)],
                own_sem.at[c, part_id],
            )
            copy.start()
            own.append(copy)

    loads = [
        pltpu.make_async_copy(src, dst, in_sem.at[i])
        for i, (src, dst) in enumerate(((q_far, q), (g_far, g)))
    ]
    for copy in loads:
        copy.start()

    barrier = pltpu.get_barrier_semaphore()
    for other in (left, right):
        pl.semaphore_signal(
            barrier, inc=1, device_id={"wide": other}, device_id_type=pl.DeviceIdType.MESH
        )
    pl.semaphore_wait(barrier, 2)

    def send(src, dst, send_sem, recv_sem, device):
        return pltpu.make_async_remote_copy(
            src_ref=src,
            dst_ref=dst,
            send_sem=send_sem,
            recv_sem=recv_sem,
            device_id={"wide": device},
            device_id_type=pl.DeviceIdType.MESH,
        )

    def span(way, short):
        return pl.ds(way * rows, rows) if short else pl.ds(0, 2 * rows)

    def gather_copy(way, c, s):
        sign = 1 - 2 * way
        block = kv.at[at(-sign * (s - 1)), c, span(way, s == half)]
        return send(
            block, block, ag_send.at[way, c, s - 1], ag_recv.at[way, c, s - 1], (right, left)[way]
        )

    def gather(c, s):
        if s == 0:
            own[2 * c].wait()
            own[2 * c + 1].wait()
        for way in range(2):
            if s > 0:
                gather_copy(way, c, s).wait_recv()
            if s < half:
                copy = gather_copy(way, c, s + 1)
                copy.start()
                copies.append(copy)

    def reduce_copy(way, c, s):
        sign = 1 - 2 * way
        part_of = span(way, s == 1)
        return send(
            part.at[at(sign * (half + 1 - s)), c, part_of],
            landed.at[way, c, s - 1, part_of],
            rs_send.at[way, c, s - 1],
            rs_recv.at[way, c, s - 1],
            (right, left)[way],
        )

    def reduce(c, s):
        for way in range(2):
            sign = 1 - 2 * way
            if s > 1:
                reduce_copy(way, c, s - 1).wait_recv()
            if s <= half:
                if s > 1:
                    part_of = span(way, s == 2)
                    target = at(sign * (half + 1 - s))
                    part[target, c, part_of] = (
                        part[target, c, part_of].astype(jnp.float32)
                        + landed[way, c, s - 2, part_of].astype(jnp.float32)
                    ).astype(bf)
                copy = reduce_copy(way, c, s)
                copy.start()
                copies.append(copy)
        if s > half:
            for part_id, ref in enumerate((pdk, pdv)):
                part_of = pl.ds(part_id * rows, rows)
                total = part[me, c, part_of].astype(jnp.float32)
                for way in range(2):
                    if half > 1 or way == part_id:
                        total += landed[way, c, half - 1, part_of].astype(jnp.float32)
                ref[:, pl.ds(c * HD, HD)] = total.astype(bf)

    lag = lambda c: max(0, c + 1 - LEAD)
    waits = sorted((lag(c) + s, c, s) for c in range(groups) for s in range(half + 1))
    for tick, c, s in [w for w in waits if w[0] == 0]:
        gather(c, s)
    waits = [w for w in waits if w[0] > 0]

    select = row_slots(prompt[...], n, capacity)
    for src, dst in ((k, ks), (v, vs)):
        dst[...] = tn(select, src[...]).astype(bf)

    def to_slots(c):
        for src, dst in ((q, qs), (g, gs)):
            dst[:, c * width : (c + 1) * width] = tn(select, src[:, c * width : (c + 1) * width]).astype(bf)

    for copy in loads:
        copy.wait()
    ready = 0

    def from_slots(c):
        for slot_ref, ref, cols in ((os, o, width), (dqs, dq, width), (dks, dk, HD), (dvs, dv, HD)):
            ref[:, c * cols : (c + 1) * cols] = nn(select, slot_ref[...]).astype(bf)

    keys = bunch * rows + slots
    mask = key_mask(keys, slots, capacity, rows, bunch)
    ahead = [half]
    for step in range(half - 1, 0, -1):
        ahead += [step, -step]
    ahead += [0]

    def tile(c, t):
        first = at(ahead[t]) if bunch == 1 else t * bunch
        place = pl.ds(pl.multiple_of(first * capacity, slots), slots)
        stack = lambda ref: jnp.concatenate(
            [ref[place, c * width + h * HD : c * width + (h + 1) * HD] for h in range(GRP)], axis=0
        )
        cols = slice(c * HD, (c + 1) * HD)
        key_block = jnp.concatenate(
            [kv[first + i, c, :rows] for i in range(bunch)] + [ks[place, cols]], axis=0
        )
        value_block = jnp.concatenate(
            [kv[first + i, c, rows:] for i in range(bunch)] + [vs[place, cols]], axis=0
        )
        out, dquery, dkey, dvalue = attend(
            stack(qs), stack(gs), key_block, value_block, mask, slots if bunch == 1 else keys, scale
        )
        for ref, value in ((os, out), (dqs, dquery)):
            for h in range(GRP):
                ref[place, h * HD : (h + 1) * HD] = value[h * slots : (h + 1) * slots].astype(bf)
        for i in range(bunch):
            piece = slice(i * rows, (i + 1) * rows)
            part[first + i, c, :rows] = dkey[piece].astype(bf)
            part[first + i, c, rows:] = dvalue[piece].astype(bf)
        dks[place, :] = dkey[bunch * rows :].astype(bf)
        dvs[place, :] = dvalue[bunch * rows :].astype(bf)

    reduces = []
    for c in range(groups):
        reduces.append((c * tiles + (0 if bunch == 1 else tiles - 1), c, 1))
        for s in range(2, half + 2):
            early = EARLY if c == groups - 1 and bunch == 1 else 0
            reduces.append((c * tiles + tiles - 1 - early + GAP * (s - 2), c, s))
    reduces.sort()

    for c in range(groups):
        while waits and waits[0][:2] <= (half + lag(c), c):
            tick, other, s = waits.pop(0)
            gather(other, s)
            if ready < groups:
                to_slots(ready)
                ready += 1
        while ready < min(groups, c + 2):
            to_slots(ready)
            ready += 1
        for t in range(tiles):
            tile(c, t)
            if t % 2 == 0 and waits and waits[0][0] <= half + lag(c):
                tick, other, s = waits.pop(0)
                gather(other, s)
            while reduces and reduces[0][0] <= c * tiles + t:
                _, other, s = reduces.pop(0)
                reduce(other, s)
        from_slots(c)
    for _, other, s in reduces:
        reduce(other, s)
    for copy in copies:
        copy.wait_send()


def write_out(*refs):
    count = (len(refs) - 1) // 2
    copies = [
        pltpu.make_async_copy(refs[i], refs[count + i], refs[-1].at[i]) for i in range(count)
    ]
    for copy in copies:
        copy.start()
    for copy in copies:
        copy.wait()


def per_device(queries, keys, values, prefix_keys, prefix_values, out_grad, row_prompt):
    n = lax.axis_size("wide")
    rows = queries.shape[0]
    prefix_rows = prefix_keys.shape[0]
    capacity = 2 * rows // n
    slots = max(32, capacity)
    places = n * capacity
    groups = keys.shape[1] // HD
    half = n // 2
    bf = jnp.bfloat16
    shape = lambda x: jax.ShapeDtypeStruct(x.shape, bf)
    vmem = pl.BlockSpec(memory_space=pltpu.VMEM)
    anywhere = pl.BlockSpec(memory_space=pl.ANY)
    sems = pltpu.SemaphoreType.DMA
    results = pl.pallas_call(
        functools.partial(kernel, n, capacity, slots, groups),
        out_shape=[shape(x) for x in (queries, queries, keys, values, prefix_keys, prefix_values)],
        in_specs=[vmem] + [anywhere] * 2 + [vmem] * 2 + [anywhere] * 2,
        out_specs=[vmem] * 6,
        scratch_shapes=[
            pltpu.VMEM(queries.shape, bf),
            pltpu.VMEM(queries.shape, bf),
            pltpu.VMEM((n, groups, 2 * prefix_rows, HD), bf),
            pltpu.VMEM((n, groups, 2 * prefix_rows, HD), bf),
            pltpu.VMEM((2, groups, half, 2 * prefix_rows, HD), bf),
            pltpu.VMEM((places, queries.shape[1]), bf),
            pltpu.VMEM((places, queries.shape[1]), bf),
            pltpu.VMEM((places, keys.shape[1]), bf),
            pltpu.VMEM((places, keys.shape[1]), bf),
            pltpu.VMEM((places, GRP * HD), bf),
            pltpu.VMEM((places, GRP * HD), bf),
            pltpu.VMEM((places, HD), bf),
            pltpu.VMEM((places, HD), bf),
            sems((2,)),
            sems((groups, 2)),
            sems((2, groups, half)),
            sems((2, groups, half)),
            sems((2, groups, half)),
            sems((2, groups, half)),
        ],
        compiler_params=pltpu.CompilerParams(collective_id=0, has_side_effects=True),
    )(row_prompt.T, queries, out_grad, keys, values, prefix_keys, prefix_values)
    return pl.pallas_call(
        write_out,
        out_shape=[shape(x) for x in results],
        in_specs=[vmem] * len(results),
        out_specs=[anywhere] * len(results),
        scratch_shapes=[sems((len(results),))],
    )(*results)


def solution(mesh):
    rows = P(("groups", "wide"), "mp")
    return jax.shard_map(
        per_device,
        mesh=mesh,
        in_specs=(rows,) * 6 + (P(("groups", "wide"), None),),
        out_specs=(rows,) * 6,
        check_vma=False,
    )
```

```python
import functools

import jax
import jax.numpy as jnp
from jax import lax
from jax.experimental import pallas as pl
from jax.experimental.pallas import tpu as pltpu
from jax.sharding import PartitionSpec as P

QH = 40
KH = 8
HD = 128
GRP = QH // KH
MASKED = -1e30
LEAD = 2
EARLY = 5
GAP = 10


def nt(a, b):
    return lax.dot_general(a, b, (((1,), (1,)), ((), ())), preferred_element_type=jnp.float32)


def nn(a, b):
    return lax.dot_general(a, b, (((1,), (0,)), ((), ())), preferred_element_type=jnp.float32)


def tn(a, b):
    return lax.dot_general(a, b, (((0,), (0,)), ((), ())), preferred_element_type=jnp.float32)


def row_slots(prompt, n_wide, capacity):
    rows = prompt.shape[1]
    lanes = max(128, n_wide)
    prompt = jnp.broadcast_to(prompt.astype(jnp.float32), (128, rows)).T[:, :1].astype(jnp.int32)
    hits = prompt == lax.broadcasted_iota(jnp.int32, (rows, lanes), 1)
    earlier = lax.broadcasted_iota(jnp.int32, (rows, rows), 1) < lax.broadcasted_iota(
        jnp.int32, (rows, rows), 0
    )
    seen = nn(
        jnp.where(earlier, 1.0, 0.0).astype(jnp.bfloat16),
        jnp.where(hits, 1.0, 0.0).astype(jnp.bfloat16),
    )
    rank = jnp.sum(jnp.where(hits, seen, 0.0), axis=1, keepdims=True)
    slot = prompt.astype(jnp.float32) * capacity + rank
    places = lax.broadcasted_iota(jnp.int32, (rows, n_wide * capacity), 1).astype(jnp.float32)
    return jnp.where(slot == places, 1.0, 0.0).astype(jnp.bfloat16)


def key_mask(keys, slots, capacity, prefix_rows, bunch):
    shape = (keys, GRP * slots)
    key = lax.broadcasted_iota(jnp.int32, shape, 0)
    row = lax.broadcasted_iota(jnp.int32, shape, 1) % slots
    own = key - bunch * prefix_rows
    same = jnp.where(own >= 0, own // capacity, key // prefix_rows) == row // capacity
    return same & (own <= row)


def attend(q, g, k, v, mask, masked_rows, scale):
    keys = k.shape[0]
    scores = nt(k, q) * scale
    if masked_rows == keys:
        scores = jnp.where(mask, scores, MASKED)
    else:
        scores = jnp.concatenate(
            [
                scores[: keys - masked_rows],
                jnp.where(mask[keys - masked_rows :], scores[keys - masked_rows :], MASKED),
            ],
            axis=0,
        )
    weights = jnp.exp(scores - jnp.max(scores, axis=0, keepdims=True))
    probs = weights * (1.0 / jnp.sum(weights, axis=0, keepdims=True))
    low = probs.astype(jnp.bfloat16)
    dprob = nt(v, g)
    weighted = probs * dprob
    delta = jnp.sum(weighted, axis=0, keepdims=True)
    dscore = (weighted - probs * delta).astype(jnp.bfloat16)
    return tn(low, v), tn(dscore, k) * scale, nn(dscore, q) * scale, nn(low, g)


def ring_index(position, count):
    half = count // 2
    position = lax.rem(position + 2 * count, count)
    return jnp.where(position < half, 2 * position, 2 * (count - 1 - position) + 1)


def ring_position(index, count):
    return jnp.where(index % 2 == 0, index // 2, count - 1 - index // 2)


def kernel(
    n, capacity, slots, groups,
    prompt, q_far, g_far, k, v, pk, pv, o, dq, dk, dv, pdk, pdv,
    q, g, kv, part, landed, qs, gs, ks, vs, os, dqs, dks, dvs,
    in_sem, own_sem, ag_send, ag_recv, rs_send, rs_recv,
):
    bf = jnp.bfloat16
    scale = HD ** (-0.5)
    half = n // 2
    bunch = slots // capacity
    tiles = n * capacity // slots
    rows = pk.shape[0]
    width = GRP * HD
    me = lax.axis_index("wide")
    here = ring_position(me, n)
    at = lambda offset: ring_index(here + offset, n)
    right, left = at(1), at(-1)
    copies = []

    own = []
    for c in range(groups):
        for part_id, ref in enumerate((pk, pv)):
            copy = pltpu.make_async_copy(
                ref.at[:, pl.ds(c * HD, HD)],
                kv.at[me, c, pl.ds(part_id * rows, rows)],
                own_sem.at[c, part_id],
            )
            copy.start()
            own.append(copy)

    loads = [
        pltpu.make_async_copy(src, dst, in_sem.at[i])
        for i, (src, dst) in enumerate(((q_far, q), (g_far, g)))
    ]
    for copy in loads:
        copy.start()

    barrier = pltpu.get_barrier_semaphore()
    for other in (left, right):
        pl.semaphore_signal(
            barrier, inc=1, device_id={"wide": other}, device_id_type=pl.DeviceIdType.MESH
        )
    pl.semaphore_wait(barrier, 2)

    def send(src, dst, send_sem, recv_sem, device):
        return pltpu.make_async_remote_copy(
            src_ref=src,
            dst_ref=dst,
            send_sem=send_sem,
            recv_sem=recv_sem,
            device_id={"wide": device},
            device_id_type=pl.DeviceIdType.MESH,
        )

    def span(way, short):
        return pl.ds(way * rows, rows) if short else pl.ds(0, 2 * rows)

    def gather_copy(way, c, s):
        sign = 1 - 2 * way
        block = kv.at[at(-sign * (s - 1)), c, span(way, s == half)]
        return send(
            block, block, ag_send.at[way, c, s - 1], ag_recv.at[way, c, s - 1], (right, left)[way]
        )

    def gather(c, s):
        if s == 0:
            own[2 * c].wait()
            own[2 * c + 1].wait()
        for way in range(2):
            if s > 0:
                gather_copy(way, c, s).wait_recv()
            if s < half:
                copy = gather_copy(way, c, s + 1)
                copy.start()
                copies.append(copy)

    def reduce_copy(way, c, s):
        sign = 1 - 2 * way
        part_of = span(way, s == 1)
        return send(
            part.at[at(sign * (half + 1 - s)), c, part_of],
            landed.at[way, c, s - 1, part_of],
            rs_send.at[way, c, s - 1],
            rs_recv.at[way, c, s - 1],
            (right, left)[way],
        )

    def reduce(c, s):
        for way in range(2):
            sign = 1 - 2 * way
            if s > 1:
                reduce_copy(way, c, s - 1).wait_recv()
            if s <= half:
                if s > 1:
                    part_of = span(way, s == 2)
                    target = at(sign * (half + 1 - s))
                    part[target, c, part_of] = (
                        part[target, c, part_of].astype(jnp.float32)
                        + landed[way, c, s - 2, part_of].astype(jnp.float32)
                    ).astype(bf)
                copy = reduce_copy(way, c, s)
                copy.start()
                copies.append(copy)
        if s > half:
            for part_id, ref in enumerate((pdk, pdv)):
                part_of = pl.ds(part_id * rows, rows)
                total = part[me, c, part_of].astype(jnp.float32)
                for way in range(2):
                    if half > 1 or way == part_id:
                        total += landed[way, c, half - 1, part_of].astype(jnp.float32)
                ref[:, pl.ds(c * HD, HD)] = total.astype(bf)

    lag = lambda c: max(0, c + 1 - LEAD)
    waits = sorted((lag(c) + s, c, s) for c in range(groups) for s in range(half + 1))
    for tick, c, s in [w for w in waits if w[0] == 0]:
        gather(c, s)
    waits = [w for w in waits if w[0] > 0]

    select = row_slots(prompt[...], n, capacity)
    for src, dst in ((k, ks), (v, vs)):
        dst[...] = tn(select, src[...]).astype(bf)

    def to_slots(c):
        for src, dst in ((q, qs), (g, gs)):
            dst[:, c * width : (c + 1) * width] = tn(select, src[:, c * width : (c + 1) * width]).astype(bf)

    for copy in loads:
        copy.wait()
    ready = 0

    def from_slots(c):
        for slot_ref, ref, cols in ((os, o, width), (dqs, dq, width), (dks, dk, HD), (dvs, dv, HD)):
            ref[:, c * cols : (c + 1) * cols] = nn(select, slot_ref[...]).astype(bf)

    keys = bunch * rows + slots
    mask = key_mask(keys, slots, capacity, rows, bunch)
    ahead = [half]
    for step in range(half - 1, 0, -1):
        ahead += [step, -step]
    ahead += [0]

    def tile(c, t):
        first = at(ahead[t]) if bunch == 1 else t * bunch
        place = pl.ds(pl.multiple_of(first * capacity, slots), slots)
        stack = lambda ref: jnp.concatenate(
            [ref[place, c * width + h * HD : c * width + (h + 1) * HD] for h in range(GRP)], axis=0
        )
        cols = slice(c * HD, (c + 1) * HD)
        key_block = jnp.concatenate(
            [kv[first + i, c, :rows] for i in range(bunch)] + [ks[place, cols]], axis=0
        )
        value_block = jnp.concatenate(
            [kv[first + i, c, rows:] for i in range(bunch)] + [vs[place, cols]], axis=0
        )
        out, dquery, dkey, dvalue = attend(
            stack(qs), stack(gs), key_block, value_block, mask, slots if bunch == 1 else keys, scale
        )
        for ref, value in ((os, out), (dqs, dquery)):
            for h in range(GRP):
                ref[place, h * HD : (h + 1) * HD] = value[h * slots : (h + 1) * slots].astype(bf)
        for i in range(bunch):
            piece = slice(i * rows, (i + 1) * rows)
            part[first + i, c, :rows] = dkey[piece].astype(bf)
            part[first + i, c, rows:] = dvalue[piece].astype(bf)
        dks[place, :] = dkey[bunch * rows :].astype(bf)
        dvs[place, :] = dvalue[bunch * rows :].astype(bf)

    reduces = []
    for c in range(groups):
        reduces.append((c * tiles + (0 if bunch == 1 else tiles - 1), c, 1))
        for s in range(2, half + 2):
            early = EARLY if c == groups - 1 and bunch == 1 else 0
            reduces.append((c * tiles + tiles - 1 - early + GAP * (s - 2), c, s))
    reduces.sort()

    for c in range(groups):
        while waits and waits[0][:2] <= (half + lag(c), c):
            tick, other, s = waits.pop(0)
            gather(other, s)
            if ready < groups:
                to_slots(ready)
                ready += 1
        while ready < min(groups, c + 2):
            to_slots(ready)
            ready += 1
        for t in range(tiles):
            tile(c, t)
            if t % 2 == 0 and waits and waits[0][0] <= half + lag(c):
                tick, other, s = waits.pop(0)
                gather(other, s)
            while reduces and reduces[0][0] <= c * tiles + t:
                _, other, s = reduces.pop(0)
                reduce(other, s)
        from_slots(c)
    for _, other, s in reduces:
        reduce(other, s)
    for copy in copies:
        copy.wait_send()


def write_out(*refs):
    count = len(refs) // 3
    sems = refs[-1]
    steps = [
        pltpu.make_async_copy(refs[a * count + i], refs[b * count + i], sems.at[k, i])
        for k, (a, b) in enumerate(((0, 2), (2, 1)))
        for i in range(count)
    ]
    for copy in steps[:count]:
        copy.start()
    for i in range(count):
        steps[i].wait()
        steps[count + i].start()
    for copy in steps[count:]:
        copy.wait()


def per_device(queries, keys, values, prefix_keys, prefix_values, out_grad, row_prompt):
    n = lax.axis_size("wide")
    rows = queries.shape[0]
    prefix_rows = prefix_keys.shape[0]
    capacity = 2 * rows // n
    slots = max(32, capacity)
    places = n * capacity
    groups = keys.shape[1] // HD
    half = n // 2
    bf = jnp.bfloat16
    shape = lambda x: jax.ShapeDtypeStruct(x.shape, bf)
    vmem = pl.BlockSpec(memory_space=pltpu.VMEM)
    anywhere = pl.BlockSpec(memory_space=pl.ANY)
    sems = pltpu.SemaphoreType.DMA
    results = pl.pallas_call(
        functools.partial(kernel, n, capacity, slots, groups),
        out_shape=[shape(x) for x in (queries, queries, keys, values, prefix_keys, prefix_values)],
        in_specs=[vmem] + [anywhere] * 2 + [vmem] * 2 + [anywhere] * 2,
        out_specs=[vmem] * 6,
        scratch_shapes=[
            pltpu.VMEM(queries.shape, bf),
            pltpu.VMEM(queries.shape, bf),
            pltpu.VMEM((n, groups, 2 * prefix_rows, HD), bf),
            pltpu.VMEM((n, groups, 2 * prefix_rows, HD), bf),
            pltpu.VMEM((2, groups, half, 2 * prefix_rows, HD), bf),
            pltpu.VMEM((places, queries.shape[1]), bf),
            pltpu.VMEM((places, queries.shape[1]), bf),
            pltpu.VMEM((places, keys.shape[1]), bf),
            pltpu.VMEM((places, keys.shape[1]), bf),
            pltpu.VMEM((places, GRP * HD), bf),
            pltpu.VMEM((places, GRP * HD), bf),
            pltpu.VMEM((places, HD), bf),
            pltpu.VMEM((places, HD), bf),
            sems((2,)),
            sems((groups, 2)),
            sems((2, groups, half)),
            sems((2, groups, half)),
            sems((2, groups, half)),
            sems((2, groups, half)),
        ],
        compiler_params=pltpu.CompilerParams(collective_id=0, has_side_effects=True),
    )(row_prompt.T, queries, out_grad, keys, values, prefix_keys, prefix_values)
    return pl.pallas_call(
        write_out,
        out_shape=[shape(x) for x in results],
        in_specs=[anywhere] * len(results),
        out_specs=[anywhere] * len(results),
        scratch_shapes=[pltpu.VMEM(x.shape, bf) for x in results] + [sems((2, len(results)))],
    )(*results)


def solution(mesh):
    rows = P(("groups", "wide"), "mp")
    return jax.shard_map(
        per_device,
        mesh=mesh,
        in_specs=(rows,) * 6 + (P(("groups", "wide"), None),),
        out_specs=(rows,) * 6,
        check_vma=False,
    )
```
